256 devices in a mesh: dp: 64 (over z, y, core), tensor: 4 (over x).
Axes of the slice: x: 4, y: 4, z: 8, core: 2. Of those that a mesh axis runs over, the one named last changes fastest.
Arguments:
- gradient: float32 [48, 1024, 1024], P(None, 'dp', 'tensor'), may hold values from -90 to 90
- second_moment: float32 [48, 1024, 1024], P(None, 'dp', 'tensor'), may hold values from 0.1 to 1
- owner_table: int32 [48], replicated, may hold values from 0 to 63, as said below
- slot_table: int32 [48], replicated, may hold values from 0 to 1, as said below
- left_stat: float32 [64, 2, 1024, 1024], P('dp', None, 'tensor'), may hold values from -1 to 4
- right_stat: float32 [64, 2, 1024, 1024], P('dp', None, 'tensor'), may hold values from -1 to 4
- left_root: bfloat16 [64, 2, 1024, 1024], P('dp', None, 'tensor'), may hold values from -1 to 4
- right_root: bfloat16 [64, 2, 1024, 1024], P('dp', None, 'tensor'), may hold values from -1 to 4
Outputs:
- update: bfloat16 [48, 1024, 1024], P(None, 'dp', 'tensor')
- new_second: float32 [48, 1024, 1024], P(None, 'dp', 'tensor')
- left_new: float32 [64, 2, 1024, 1024], P('dp', None, 'tensor')
- right_new: float32 [64, 2, 1024, 1024], P('dp', None, 'tensor')
The draws below stay inside these ranges and needn't reach their ends.
Inputs may be any that keep to these rules, and one draw needn't show every extreme that they name: The pairs (owner_table[b], slot_table[b]) are distinct; each owner holds at most 2 blocks, and some owner holds exactly 2; owners 0 and 63 each hold at least one block. `slot_table`: paired with owner_table as stated there.
All inputs are finite; a program needn't handle non-finite values.
Results may differ from the reference program's by a relative error of at most 0.0064.
Values may be sent and summed in bfloat16 or wider, within the bound.
A program may use at most 64 MiB of HBM per device.

```python
import math
import jax
import jax.numpy as jnp
from jax import lax

BLOCK = 1024
SLOTS = 2
OWNERS = 64
BLOCKS = 48


def assignment(key):
    base = jax.random.fold_in(key, 7)
    shuffled = jax.random.permutation(base, OWNERS * SLOTS)
    full_owner = shuffled[0] // SLOTS
    picked_slot = shuffled[1] % SLOTS
    positions = jnp.arange(OWNERS * SLOTS, dtype=jnp.int32)
    ranking = jnp.argsort(shuffled).astype(jnp.int32)
    forced = (positions // SLOTS == full_owner) | (positions == picked_slot) | (positions == (OWNERS - 1) * SLOTS + picked_slot)
    scores = jnp.where(forced, -1, ranking)
    ordered = jnp.argsort(scores, stable=True).astype(jnp.int32)
    chosen = ordered[:BLOCKS]
    mixing = jax.random.permutation(jax.random.fold_in(key, 8), BLOCKS)
    chosen = chosen[mixing]
    return ((chosen // SLOTS).astype(jnp.int32), (chosen % SLOTS).astype(jnp.int32))


def draw_owner_table(key, part):
    return assignment(key)[0]


def draw_slot_table(key, part):
    return assignment(key)[1]


def dominant(key, low_diag, high_diag):
    keys = jax.random.split(key, 2)
    noise = jax.random.normal(keys[0], (OWNERS, SLOTS, BLOCK, BLOCK), jnp.float32) * (0.7 / math.sqrt(2.0 * BLOCK))
    noise = jnp.clip(noise, -6.0 * 0.7 / math.sqrt(2.0 * BLOCK), 6.0 * 0.7 / math.sqrt(2.0 * BLOCK))
    noise = noise + jnp.swapaxes(noise, 2, 3)
    diagonal = jax.random.uniform(keys[1], (OWNERS, SLOTS, BLOCK, 1), jnp.float32, low_diag, high_diag)
    identity = (jnp.arange(BLOCK)[:, None] == jnp.arange(BLOCK)[None, :]).astype(jnp.float32)
    return noise + identity * diagonal


def draw_left_stat(key, part):
    return dominant(jax.random.fold_in(key, 1), 0.5, 3.0)


def draw_right_stat(key, part):
    return dominant(jax.random.fold_in(key, 2), 0.5, 3.0)


def draw_left_root(key, part):
    return dominant(jax.random.fold_in(key, 3), 0.5, 1.5).astype(jnp.bfloat16)


def draw_right_root(key, part):
    return dominant(jax.random.fold_in(key, 4), 0.5, 1.5).astype(jnp.bfloat16)


def draw_gradient(key, part):
    keys = jax.random.split(key, 3)
    shape = (BLOCKS, BLOCK, BLOCK)
    base = jnp.clip(jax.random.normal(keys[0], shape, jnp.float32), -6.0, 6.0)
    row_scale = jnp.exp(jax.random.uniform(keys[1], (BLOCKS, BLOCK, 1), jnp.float32) * math.log(10.0))
    col_scale = jnp.exp(jax.random.uniform(keys[2], (BLOCKS, 1, BLOCK), jnp.float32) * math.log(10.0))
    rising = 1.0 + 2.0 * jnp.arange(BLOCK, dtype=jnp.float32)[None, :, None] / BLOCK
    return 0.05 * base * row_scale * col_scale * rising


def block_levels(own_key, extent, shards, low, high):
    loudness = 1.0
    for position, parts in shards:
        steps = jax.random.uniform(jax.random.fold_in(jax.random.fold_in(own_key, 6), position), (parts,), jnp.float32, low / len(shards), high / len(shards))
        loudness = loudness * jnp.repeat(jnp.exp(steps), extent[position] // parts).reshape((-1,) + (1,) * (len(extent) - 1 - position))
    return loudness


def setup_inputs(seed: int = 0) -> dict:
    key_of = jax.random.split(jax.random.key(seed), 9)
    gradient = draw_gradient(jax.random.fold_in(key_of[8], 71), 0)
    second_moment = jnp.clip(jnp.exp(math.log(1.0) - 2.3025851 * jax.random.uniform(key_of[1], (BLOCKS, BLOCK, BLOCK), jnp.float32) ** block_levels(key_of[1], (BLOCKS, BLOCK, BLOCK), ((1, 64), (2, 4)), -0.2, 0.2)), 0.1, 1.0)
    owner_table = draw_owner_table(jax.random.fold_in(key_of[8], 71), 0)
    slot_table = draw_slot_table(jax.random.fold_in(key_of[8], 71), 0)
    left_stat = draw_left_stat(jax.random.fold_in(key_of[8], 71), 0)
    right_stat = draw_right_stat(jax.random.fold_in(key_of[8], 71), 0)
    left_root = draw_left_root(jax.random.fold_in(key_of[8], 71), 0)
    right_root = draw_right_root(jax.random.fold_in(key_of[8], 71), 0)
    return {"gradient": gradient, "second_moment": second_moment, "owner_table": owner_table, "slot_table": slot_table, "left_stat": left_stat, "right_stat": right_stat, "left_root": left_root, "right_root": right_root}


def precondition_block(operands):
    grad_block, lroot, rroot = operands
    left_term = jnp.dot(grad_block, grad_block.T, preferred_element_type=jnp.float32)
    right_term = jnp.dot(grad_block.T, grad_block, preferred_element_type=jnp.float32)
    mixed = jnp.dot(lroot, grad_block, preferred_element_type=jnp.float32).astype(jnp.bfloat16)
    precond = jnp.dot(mixed, rroot, preferred_element_type=jnp.float32).astype(jnp.bfloat16)
    return (left_term, right_term, precond)

def reference(gradient, second_moment, owner_table, slot_table, left_stat, right_stat, left_root, right_root):
    flat_index = (owner_table * SLOTS + slot_table).astype(jnp.int32)
    new_second = 0.99 * second_moment + 0.01 * gradient * gradient
    adam = gradient / (jnp.sqrt(new_second) + 1e-08)
    adam_norm = lax.optimization_barrier(jnp.sum(adam * adam, axis=(1, 2)))
    grad_low = gradient.astype(jnp.bfloat16)
    lroots = left_root.reshape(OWNERS * SLOTS, BLOCK, BLOCK)[flat_index]
    rroots = right_root.reshape(OWNERS * SLOTS, BLOCK, BLOCK)[flat_index]
    left_terms, right_terms, precond = lax.map(precondition_block, (grad_low, lroots, rroots))
    left_flat = 0.5 * left_stat.reshape(OWNERS * SLOTS, BLOCK, BLOCK)
    right_flat = 0.5 * right_stat.reshape(OWNERS * SLOTS, BLOCK, BLOCK)
    left_new = left_flat.at[flat_index].add(0.5 / BLOCK * left_terms).reshape(OWNERS, SLOTS, BLOCK, BLOCK)
    right_new = right_flat.at[flat_index].add(0.5 / BLOCK * right_terms).reshape(OWNERS, SLOTS, BLOCK, BLOCK)
    precond_wide = precond.astype(jnp.float32)
    root_norm = lax.optimization_barrier(jnp.sum(precond_wide * precond_wide, axis=(1, 2)))
    graft_scale = jnp.sqrt(adam_norm / (root_norm + 1e-06))
    update = (graft_scale[:, None, None] * precond_wide).astype(jnp.bfloat16)
    return (update, new_second, left_new, right_new)
```

```python
import functools

import jax
import jax.numpy as jnp
from jax import lax
from jax.experimental import pallas as pl
from jax.experimental.pallas import tpu as pltpu
from jax.sharding import PartitionSpec as P

MESH = pl.DeviceIdType.MESH
NX, NY, NZ, NC = 4, 4, 8, 2


def position():
    dp = lax.axis_index("dp")
    x = lax.axis_index("tensor")
    return x, (dp // NC) % NY, dp // (NC * NY), dp % NC


def device(x, y, z, c):
    return ((z * NY + y) * NC + c, x)


def entry_barrier(x, y, z, c):
    barrier = pltpu.get_barrier_semaphore()
    partners = [(x, y, (z + k) % NZ, c) for k in range(1, NZ)]
    partners += [(x, (y + k) % NY, z, c) for k in range(1, NY)]
    partners += [((x + k) % NX, y, z, h) for k in range(1, NX) for h in range(NC)]
    partners += [(x, y, z, 1 - c)]
    for partner in partners:
        pl.semaphore_signal(barrier, inc=1, device_id=device(*partner), device_id_type=MESH)
    pl.semaphore_wait(barrier, len(partners))


def remote(src, dst, send_sem, recv_sem, target):
    return pltpu.make_async_remote_copy(
        src_ref=src,
        dst_ref=dst,
        send_sem=send_sem,
        recv_sem=recv_sem,
        device_id=device(*target),
        device_id_type=MESH,
    )


def either(is_self, src, dst, send_sem, recv_sem, target):
    @pl.when(is_self)
    def _():
        pltpu.make_async_copy(src, dst, recv_sem).start()

    @pl.when(jnp.logical_not(is_self))
    def _():
        remote(src, dst, send_sem, recv_sem, target).start()


Z_ORDER = (4, 3, 5, 2, 6, 1, 7)
Y_ORDER = (2, 1, 3)
IN_ORDER = (2, 1, 3, 0)
OUT_ORDER = (0, 1, 3, 2)


def gather_kernel(
    slots, lroot, rroot, whole, left, right, zr, yr,
    z_send, z_recv, y_send, y_recv, x_send, x_recv, c_send, c_recv,
    l_send, l_recv, r_send, r_recv, f_send, f_recv,
):
    x, y, z, c = position()
    entry_barrier(x, y, z, c)
    width = slots.shape[4]

    def z_copy(j, k):
        to = (z + k) % NZ
        return remote(
            slots.at[to, :, (x + j) % NX], zr.at[j, :, z],
            z_send.at[j, k], z_recv.at[j, k], (x, y, to, c),
        )

    def z_own(j):
        return pltpu.make_async_copy(slots.at[z, :, (x + j) % NX], zr.at[j, :, z], z_recv.at[j, 0])

    def y_copy(j, k):
        to = (y + k) % NY
        return remote(
            zr.at[j, to], yr.at[j, :, y], y_send.at[j, k], y_recv.at[j, k], (x, to, z, c)
        )

    def y_own(j):
        return pltpu.make_async_copy(zr.at[j, y], yr.at[j, :, y], y_recv.at[j, 0])

    def cols(index):
        return pl.ds(pl.multiple_of(index * width, width), width)

    def x_copy(j):
        to = (x + j) % NX
        return remote(
            yr.at[j], whole.at[:, :, c, :, cols(x)],
            x_send.at[j], x_recv.at[j], (to, y, z, c),
        )

    def x_own():
        return pltpu.make_async_copy(yr.at[0], whole.at[:, :, c, :, cols(x)], x_recv.at[0])

    def c_copy(j):
        part = whole.at[:, :, c, :, cols((x - j + NX) % NX)]
        return remote(part, part, c_send.at[j], c_recv.at[j], (x, y, z, 1 - c))

    def root_args(s, h):
        to = NC * c + s
        is_self = jnp.logical_and(to == x, c == h)
        return is_self, to

    def forward(i):
        part = right.at[i, c]
        return remote(part, part, f_send.at[i], f_recv.at[i], (x, y, z, 1 - c))

    for k in Z_ORDER:
        z_copy(IN_ORDER[0], k).start()
    z_own(IN_ORDER[0]).start()
    for s in range(2):
        for h in range(NC):
            is_self, to = root_args(s, h)
            either(is_self, lroot.at[s, :, h], left.at[x], l_send.at[s, h], l_recv.at[x], (to, y, z, h))
    for s in range(2):
        for h in range(NC):
            is_self, to = root_args(s, h)
            either(is_self, rroot.at[s, h], right.at[x, h], r_send.at[s, h], r_recv.at[x], (to, y, z, h))
    for j in IN_ORDER[1:]:
        for k in Z_ORDER:
            z_copy(j, k).start()
        z_own(j).start()

    def finish_y(j):
        for k in Y_ORDER:
            y_copy(j, k).wait_recv()
        y_own(j).wait()
        if j == 0:
            x_own().start()
        else:
            x_copy(j).start()

    def finish_x(j):
        if j == 0:
            x_own().wait()
        else:
            x_copy(j).wait_recv()
        c_copy(j).start()

    for i, j in enumerate(IN_ORDER):
        for k in Z_ORDER:
            z_copy(j, k).wait_recv()
        z_own(j).wait()
        for k in Y_ORDER:
            y_copy(j, k).start()
        y_own(j).start()
        if i >= 1:
            finish_y(IN_ORDER[i - 1])
    finish_y(IN_ORDER[-1])
    for i in range(NX):
        pltpu.make_async_copy(right.at[i, c], right.at[i, c], r_recv.at[i]).wait()
        forward(i).start()
    for j in IN_ORDER:
        finish_x(j)
    for i in range(NX):
        pltpu.make_async_copy(left.at[i], left.at[i], l_recv.at[i]).wait()
        forward(i).wait()
    for j in IN_ORDER:
        c_copy(j).wait()
        if j != 0:
            x_copy(j).wait_send()
        for k in Y_ORDER:
            y_copy(j, k).wait_send()
        for k in Z_ORDER:
            z_copy(j, k).wait_send()
    for s in range(2):
        for h in range(NC):
            is_self, to = root_args(s, h)

            @pl.when(jnp.logical_not(is_self))
            def _():
                remote(lroot.at[s, :, h], left.at[x], l_send.at[s, h], l_recv.at[x], (to, y, z, h)).wait_send()
                remote(rroot.at[s, h], right.at[x, h], r_send.at[s, h], r_recv.at[x], (to, y, z, h)).wait_send()


def scatter_kernel(
    precond, lterm, rterm, row, back, left, right, rows, xr, yr,
    z_send, z_recv, y_send, y_recv, x_send, x_recv,
    l_send, l_recv, r_send, r_recv, n_send, n_recv,
):
    x, y, z, c = position()
    entry_barrier(x, y, z, c)
    width = back.shape[4]

    def cols(index):
        return pl.ds(pl.multiple_of(index * width, width), width)

    def x_copy(j):
        to = (x + j) % NX
        return remote(
            precond.at[:, :, :, cols(to)], xr.at[j], x_send.at[j], x_recv.at[j], (to, y, z, c)
        )

    def x_own():
        return pltpu.make_async_copy(precond.at[:, :, :, cols(x)], xr.at[0], x_recv.at[0])

    def y_copy(j, k):
        to = (y + k) % NY
        return remote(
            xr.at[j, :, to], yr.at[j, :, y], y_send.at[j, k], y_recv.at[j, k], (x, to, z, c)
        )

    def y_own(j):
        return pltpu.make_async_copy(xr.at[j, :, y], yr.at[j, :, y], y_recv.at[j, 0])

    def z_copy(j, k):
        to = (z + k) % NZ
        return remote(
            yr.at[j, to], back.at[z, :, (x - j + NX) % NX],
            z_send.at[j, k], z_recv.at[j, k], (x, y, to, c),
        )

    def z_own(j):
        return pltpu.make_async_copy(yr.at[j, z], back.at[z, :, (x - j + NX) % NX], z_recv.at[j, 0])

    def n_copies(stage):
        if stage == 0:
            src = dst = rows.at[c, x, y, z]
            targets = [(x, y, (z + k) % NZ, c) for k in range(1, NZ)]
        elif stage == 1:
            src = dst = rows.at[c, x, y]
            targets = [(x, (y + k) % NY, z, c) for k in range(1, NY)]
        elif stage == 2:
            src = dst = rows.at[c, x]
            targets = [((x + k) % NX, y, z, c) for k in range(1, NX)]
        else:
            src = dst = rows.at[c]
            targets = [(x, y, z, 1 - c)]
        return [
            remote(src, dst, n_send.at[stage, i], n_recv.at[stage, i], target)
            for i, target in enumerate(targets)
        ]

    own_row = pltpu.make_async_copy(row, rows.at[c, x, y, z], n_recv.at[0, NZ - 1])
    own_row.start()
    x_own().start()
    for j in OUT_ORDER[1:]:
        x_copy(j).start()
    owner = x // 2
    slot = x % 2
    for i in range(1, NX + 1):
        to = (x + i) % NX
        is_self = jnp.logical_and(to == x, c == owner)
        either(is_self, lterm.at[to], left.at[slot, :, c], l_send.at[i - 1], l_recv.at[x, c], (to, y, z, owner))
    for i in range(2):
        to = NC * c + i
        is_self = jnp.logical_and(to == x, c == owner)
        either(is_self, rterm.at[i], right.at[slot], r_send.at[i], r_recv.at[slot], (to, y, z, owner))
    own_row.wait()
    for copy in n_copies(0):
        copy.start()

    def finish_y(j):
        for k in Y_ORDER:
            y_copy(j, k).wait_recv()
        y_own(j).wait()
        for k in Z_ORDER:
            z_copy(j, k).start()
        z_own(j).start()

    for i, j in enumerate(OUT_ORDER):
        if j == 0:
            x_own().wait()
        else:
            x_copy(j).wait_recv()
        for k in Y_ORDER:
            y_copy(j, k).start()
        y_own(j).start()
        if i >= 1:
            finish_y(OUT_ORDER[i - 1])
        for copy in n_copies(i):
            copy.wait_recv()
        if i < 3:
            for copy in n_copies(i + 1):
                copy.start()
    finish_y(OUT_ORDER[-1])
    for i in range(2):
        for h in range(NC):
            part = left.at[i, :, h]
            pltpu.make_async_copy(part, part, l_recv.at[NC * c + i, h]).wait()
        part = right.at[i]
        pltpu.make_async_copy(part, part, r_recv.at[i]).wait()
    for j in OUT_ORDER:
        for k in Z_ORDER:
            z_copy(j, k).wait()
        z_own(j).wait()
        for k in Y_ORDER:
            y_copy(j, k).wait_send()
        if j != 0:
            x_copy(j).wait_send()
    for stage in range(4):
        for copy in n_copies(stage):
            copy.wait_send()
    for i in range(1, NX + 1):
        to = (x + i) % NX

        @pl.when(jnp.logical_not(jnp.logical_and(to == x, c == owner)))
        def _():
            remote(lterm.at[to], left.at[slot, :, c], l_send.at[i - 1], l_recv.at[x, c], (to, y, z, owner)).wait_send()

    for i in range(2):
        to = NC * c + i

        @pl.when(jnp.logical_not(jnp.logical_and(to == x, c == owner)))
        def _():
            remote(rterm.at[i], right.at[slot], r_send.at[i], r_recv.at[slot], (to, y, z, owner)).wait_send()


ANY = pl.BlockSpec(memory_space=pl.ANY)
VMEM = pl.BlockSpec(memory_space=pltpu.VMEM)
DMA = pltpu.SemaphoreType.DMA


def per_device(
    gradient, second_moment, owner_table, slot_table, left_stat, right_stat, left_root, right_root
):
    blocks, rows, width = gradient.shape
    order = left_stat.shape[3]
    stripe = left_stat.shape[2]
    low = jnp.bfloat16
    slots = NZ * NY * NC * 2
    x, y, z, c = position()
    flat = owner_table * 2 + slot_table

    new_second = 0.99 * second_moment + 0.01 * gradient * gradient
    adam = gradient / (jnp.sqrt(new_second) + 1e-08)
    adam_part = jnp.sum(adam * adam, axis=(1, 2))
    grad_low = gradient.astype(low)
    match = flat[None, :] == jnp.arange(slots, dtype=jnp.int32)[:, None]
    taken = jnp.any(match, axis=1)
    source = jnp.sum(jnp.where(match, jnp.arange(blocks, dtype=jnp.int32)[None, :], 0), axis=1)
    slot_grad = jnp.where(taken[:, None, None], grad_low[source], jnp.zeros((), low))

    groups = stripe // (NC * rows)
    shape = jax.ShapeDtypeStruct
    whole, lroot, rroot = pl.pallas_call(
        gather_kernel,
        out_shape=(
            shape((NZ, NY, NC, rows, order), low),
            shape((NX, groups, rows, order), low),
            shape((NX, NC, stripe // NC, order), low),
        ),
        in_specs=[VMEM] * 3,
        out_specs=(ANY, ANY, ANY),
        scratch_shapes=[
            pltpu.VMEM((NX, NY, NZ, rows, width), low),
            pltpu.VMEM((NX, NZ, NY, rows, width), low),
            DMA((NX, NZ)), DMA((NX, NZ)), DMA((NX, NY)), DMA((NX, NY)),
            DMA((NX,)), DMA((NX,)), DMA((NX,)), DMA((NX,)),
            DMA((2, NC)), DMA((NX,)), DMA((2, NC)), DMA((NX,)), DMA((NX,)), DMA((NX,)),
        ],
        compiler_params=pltpu.CompilerParams(collective_id=0, has_side_effects=True),
        name="gather_blocks",
    )(
        slot_grad.reshape(NZ, NY, NX, rows, width),
        left_root.reshape(2, groups, NC, rows, order),
        right_root.reshape(2, NC, stripe // NC, order),
    )

    block = whole.reshape(order, order)
    half = order // NC
    own_rows = lax.dynamic_index_in_dim(whole, c, 2, False).reshape(half, order)
    own_cols = lax.dynamic_slice_in_dim(block, c * half, half, 1)
    dot = functools.partial(lax.dot_general, preferred_element_type=jnp.float32)
    mixed = dot(lroot.reshape(half, order), block, (((1,), (0,)), ((), ()))).astype(low)
    precond = dot(mixed, rroot.reshape(order, order), (((1,), (0,)), ((), ()))).astype(low)
    wide = precond.astype(jnp.float32)
    root_part = jnp.sum(wide * wide)
    factor = 0.5 / order
    lterm = (factor * dot(own_rows, block, (((1,), (1,)), ((), ())))).astype(low)
    rterm = (factor * dot(own_cols, block, (((0,), (0,)), ((), ())))).astype(low)

    row = jnp.concatenate(
        [adam_part, jnp.full((1,), root_part), jnp.zeros((128 - blocks - 1,), jnp.float32)]
    ).reshape(1, 128)
    back, left_term, right_term, all_rows = pl.pallas_call(
        scatter_kernel,
        out_shape=(
            shape((NZ, NY, NX, rows, width), low),
            shape((2, groups, NC, rows, order), low),
            shape((2, stripe, order), low),
            shape((NC, NX, NY, NZ, 1, 128), jnp.float32),
        ),
        in_specs=[VMEM] * 4,
        out_specs=(ANY,) * 4,
        scratch_shapes=[
            pltpu.VMEM((NX, NZ, NY, rows, width), low),
            pltpu.VMEM((NX, NZ, NY, rows, width), low),
            DMA((NX, NZ)), DMA((NX, NZ)), DMA((NX, NY)), DMA((NX, NY)),
            DMA((NX,)), DMA((NX,)),
            DMA((NX,)), DMA((NX, NC)), DMA((2,)), DMA((2,)),
            DMA((4, NZ)), DMA((4, NZ)),
        ],
        compiler_params=pltpu.CompilerParams(collective_id=1, has_side_effects=True),
        name="scatter_blocks",
    )(
        precond.reshape(NZ, NY, rows, order),
        lterm.reshape(NX, groups, rows, order),
        rterm.reshape(2, stripe, order),
        row,
    )

    left_new = 0.5 * left_stat + left_term.reshape(left_stat.shape).astype(jnp.float32)
    right_new = 0.5 * right_stat + right_term.reshape(right_stat.shape).astype(jnp.float32)
    adam_total = jnp.sum(all_rows[..., :blocks], axis=(0, 1, 2, 3, 4))
    root_slot = jnp.sum(all_rows[..., 0, blocks], axis=0).transpose(2, 1, 0).reshape(1, slots)
    root_total = jnp.sum(jnp.where(match.T, root_slot, 0.0), axis=1)
    scale = jnp.sqrt(adam_total / (root_total + 1e-06))
    returned = back.reshape(slots, rows, width)[flat]
    update = (scale[:, None, None] * returned.astype(jnp.float32)).astype(low)
    return (update, new_second, left_new, right_new)


def solution(mesh):
    placed = (
        P(None, "dp", "tensor"),
        P(None, "dp", "tensor"),
        P(),
        P(),
        P("dp", None, "tensor", None),
        P("dp", None, "tensor", None),
        P("dp", None, "tensor", None),
        P("dp", None, "tensor", None),
    )
    return jax.shard_map(
        per_device,
        mesh=mesh,
        in_specs=placed,
        out_specs=(
            P(None, "dp", "tensor"),
            P(None, "dp", "tensor"),
            P("dp", None, "tensor", None),
            P("dp", None, "tensor", None),
        ),
        check_vma=False,
    )
```

```python
import functools

import jax
import jax.numpy as jnp
from jax import lax
from jax.experimental import pallas as pl
from jax.experimental.pallas import tpu as pltpu
from jax.sharding import PartitionSpec as P

MESH = pl.DeviceIdType.MESH
NX, NY, NZ, NC = 4, 4, 8, 2


def position():
    dp = lax.axis_index("dp")
    x = lax.axis_index("tensor")
    return x, (dp // NC) % NY, dp // (NC * NY), dp % NC


def device(x, y, z, c):
    return ((z * NY + y) * NC + c, x)


def entry_barrier(x, y, z, c):
    barrier = pltpu.get_barrier_semaphore()
    partners = [(x, y, (z + k) % NZ, c) for k in range(1, NZ)]
    partners += [(x, (y + k) % NY, z, c) for k in range(1, NY)]
    partners += [((x + k) % NX, y, z, h) for k in range(1, NX) for h in range(NC)]
    partners += [(x, y, z, 1 - c)]
    for partner in partners:
        pl.semaphore_signal(barrier, inc=1, device_id=device(*partner), device_id_type=MESH)
    pl.semaphore_wait(barrier, len(partners))


def remote(src, dst, send_sem, recv_sem, target):
    return pltpu.make_async_remote_copy(
        src_ref=src,
        dst_ref=dst,
        send_sem=send_sem,
        recv_sem=recv_sem,
        device_id=device(*target),
        device_id_type=MESH,
    )


Z_ORDER = (4, 3, 5, 2, 6, 1, 7)
RING = (2, 1, 3)
IN_ORDER = (2, 1, 3, 0)
OUT_ORDER = (0, 1, 3, 2)
LOW = jnp.bfloat16
FULL = jnp.float32


def front_kernel(rank, gradient, second_moment, new_second, send, row):
    step = pl.program_id(0)
    blocks = gradient.shape[0]
    g = gradient[...]
    refreshed = 0.99 * second_moment[...] + 0.01 * g * g
    new_second[...] = refreshed
    adam = g / (jnp.sqrt(refreshed) + 1e-08)
    total = jnp.sum(jnp.sum(adam * adam, axis=1), axis=1, keepdims=True)
    low = g.astype(LOW)
    for b in range(blocks):
        place = rank[step * blocks + b]
        send[place % NX, place // NX] = low[b]
    lane = lax.broadcasted_iota(jnp.int32, (blocks, 128), 1)
    block = lax.broadcasted_iota(jnp.int32, (blocks, 128), 0) + step * blocks
    part = jnp.sum(jnp.where(lane == block, total, 0.0), axis=0, keepdims=True)

    @pl.when(step == 0)
    def _():
        row[...] = jnp.zeros_like(row)

    row[...] += part


def step_kernel(
    table, send, lroot, rroot, adam_row,
    fin, left_out, right_out, rows,
    xr, slots, zr, whole, lall, lsel, lhalf, rall, rsel, rwhole,
    mixed, precond, yr, back, xs, cols_t, lterm, rterm, norm,
    gx_send, gx_recv, gz_send, gz_recv, gy_send, gy_recv, gc_send, gc_recv,
    e_send, e_recv, l_send, l_recv, r_send, r_recv, f_send, f_recv,
    py_send, py_recv, pz_send, pz_recv, px_send, px_recv,
    dl_send, dl_recv, dr_send, dr_recv, df_send, df_recv, n_send, n_recv,
):
    x, y, z, c = position()
    entry_barrier(x, y, z, c)
    per_worker, rows_each, order = xr.shape
    width = order // NX
    half = order // NC
    sibling = (x, y, z, 1 - c)
    local = pltpu.make_async_copy

    def cols(index, size=width):
        return pl.ds(pl.multiple_of(index * size, size), size)

    def gx(k):
        to = (x + k) % NX
        return remote(send.at[to], xr.at[:, :, cols(x)], gx_send.at[k], gx_recv.at[k], (to, y, z, c))

    gx_own = local(send.at[x], xr.at[:, :, cols(x)], gx_recv.at[0])
    for k in RING:
        gx(k).start()
    gx_own.start()

    def exchange(s):
        return (
            remote(lroot.at[s, :, 1 - c], lall.at[NC * c + s], e_send.at[0, s], e_recv.at[0, s], sibling),
            remote(rroot.at[s, 1 - c], rall.at[NC * c + s], e_send.at[1, s], e_recv.at[1, s], sibling),
            local(lroot.at[s, :, c], lall.at[NC * c + s], e_recv.at[2, s]),
            local(rroot.at[s, c], rall.at[NC * c + s], e_recv.at[3, s]),
        )

    for s in range(2):
        for copy in exchange(s):
            copy.start()

    for k in RING:
        gx(k).wait_recv()
    gx_own.wait()

    def gz(m, k):
        to = (z + k) % NZ
        dst = whole.at[z, y, c] if m == 0 else zr.at[m, z]
        return remote(slots.at[m, to], dst, gz_send.at[m, k], gz_recv.at[m, k], (x, y, to, c))

    def gz_own(m):
        return local(slots.at[m, z], whole.at[z, y, c] if m == 0 else zr.at[m, z], gz_recv.at[m, 0])

    def gy(m):
        to = (y + m) % NY
        return remote(zr.at[m], whole.at[:, y, c], gy_send.at[m], gy_recv.at[m], (x, to, z, c))

    def gc(m):
        part = whole.at[:, (y - m + NY) % NY, c]
        return remote(part, part, gc_send.at[m], gc_recv.at[m], sibling)

    def build(m):
        to = (y + m) % NY

        def fill(i, carry):
            slots[m, i] = xr[table[i * NY + to]]
            return carry

        lax.fori_loop(0, NZ, fill, 0)
        for k in Z_ORDER:
            gz(m, k).start()
        gz_own(m).start()

    build(IN_ORDER[0])
    for s in range(2):
        a, b, d, e = exchange(s)
        a.wait_recv()
        b.wait_recv()
        d.wait()
        e.wait()

    def pick(i, carry):
        chosen = table[32 + i]
        lsel[i] = lall[chosen]
        rsel[i] = rall[chosen]
        return carry

    lax.fori_loop(0, NX, pick, 0)

    def lx(k):
        to = (x + k) % NX
        return remote(lsel.at[to], lhalf.at[x], l_send.at[k], l_recv.at[k], (to, y, z, c))

    def rx(k):
        to = (x + k) % NX
        return remote(rsel.at[to], rwhole.at[x, c], r_send.at[k], r_recv.at[k], (to, y, z, c))

    lx_own = local(lsel.at[x], lhalf.at[x], l_recv.at[0])
    rx_own = local(rsel.at[x], rwhole.at[x, c], r_recv.at[0])

    def forward(k):
        part = rwhole.at[(x - k + NX) % NX, c]
        return remote(part, part, f_send.at[k], f_recv.at[k], sibling)

    for k in RING:
        lx(k).start()
    lx_own.start()
    for k in RING:
        rx(k).start()
    rx_own.start()
    for m in IN_ORDER[1:]:
        build(m)

    def finish_y(m):
        gy(m).wait_recv()
        gc(m).start()

    rx_own.wait()
    forward(0).start()
    for i, m in enumerate(IN_ORDER):
        for k in Z_ORDER:
            gz(m, k).wait_recv()
        gz_own(m).wait()
        if m == 0:
            gc(0).start()
        else:
            gy(m).start()
        if i >= 1:
            finish_y(IN_ORDER[i - 1])
    for k in RING:
        rx(k).wait_recv()
        forward(k).start()
    for k in RING:
        lx(k).wait_recv()
    lx_own.wait()
    for m in IN_ORDER:
        gc(m).wait_recv()

    def dot(a, b, dims):
        return lax.dot_general(a, b, (dims, ((), ())), preferred_element_type=FULL)

    tiles = order // width

    def mix(n, carry):
        g = whole[:, :, :, :, cols(n)].reshape(order, width)
        mixed[:, cols(n)] = dot(lhalf[...].reshape(half, order), g, ((1,), (0,))).astype(LOW)
        return carry

    lax.fori_loop(0, tiles, mix, 0)
    for k in (0,) + RING:
        forward(k).wait_recv()

    def condition(n, carry):
        r = rwhole[:, :, :, cols(n)].reshape(order, width)
        p = dot(mixed[...], r, ((1,), (0,))).astype(LOW)
        precond[:, :, :, cols(n)] = p.reshape(NZ, NY, rows_each, width)
        wide = p.astype(FULL)
        return carry + jnp.sum(wide * wide, axis=0, keepdims=True)

    squares = lax.fori_loop(0, tiles, condition, jnp.zeros((1, width), FULL))

    def py(m):
        to = (y + m) % NY
        return remote(precond.at[:, to], yr.at[m], py_send.at[m], py_recv.at[m], (x, to, z, c))

    def pz(m, k):
        to = (z + k) % NZ
        src = precond.at[to, y] if m == 0 else yr.at[m, to]
        dst = back.at[z * NY + (y - m + NY) % NY]
        return remote(src, dst, pz_send.at[m, k], pz_recv.at[m, k], (x, y, to, c))

    def pz_own(m):
        src = precond.at[z, y] if m == 0 else yr.at[m, z]
        return local(src, back.at[z * NY + (y - m + NY) % NY], pz_recv.at[m, 0])

    def send_z(m):
        for k in Z_ORDER:
            pz(m, k).start()
        pz_own(m).start()

    def n_copies(stage):
        if stage == 0:
            part = rows.at[c, z, y, x]
            targets = [((x + k) % NX, y, z, c) for k in range(1, NX)]
        elif stage == 1:
            part = rows.at[c, z, y]
            targets = [(x, (y + k) % NY, z, c) for k in range(1, NY)]
        elif stage == 2:
            part = rows.at[c, z]
            targets = [(x, y, (z + k) % NZ, c) for k in range(1, NZ)]
        else:
            part = rows.at[c]
            targets = [sibling]
        return [
            remote(part, part, n_send.at[stage, i], n_recv.at[stage, i], target)
            for i, target in enumerate(targets)
        ]

    def n_step(stage):
        if stage > 0:
            for copy in n_copies(stage - 1):
                copy.wait_recv()
        if stage < 4:
            for copy in n_copies(stage):
                copy.start()

    for m in OUT_ORDER[1:]:
        py(m).start()
    send_z(0)
    norm[0:1, :] = adam_row[...]
    norm[1:2, :] = jnp.broadcast_to(jnp.sum(squares, axis=1, keepdims=True), (1, 128))
    n_own = local(norm, rows.at[c, z, y, x], n_recv.at[0, NZ - 1])
    n_own.start()
    n_own.wait()
    n_step(0)

    factor = 0.5 / order

    def gram_left(n, carry):
        own = whole[:, :, c].reshape(half, order)
        other = whole[pl.ds(n * NC, NC)].reshape(width, order)
        term = (factor * dot(own, other, ((1,), (1,)))).astype(LOW)
        lterm[:, :, :, cols(n)] = term.reshape(NX, half // (NX * rows_each), rows_each, width)
        return carry

    lax.fori_loop(0, tiles, gram_left, 0)

    def dlx(k):
        to = (x + k) % NX
        return remote(lterm.at[to], left_out.at[x, c], dl_send.at[k], dl_recv.at[k], (to, y, z, c))

    def drx(k):
        to = (x + k) % NX
        return remote(rterm.at[to], right_out.at[x, c], dr_send.at[k], dr_recv.at[k], (to, y, z, c))

    dl_own = local(lterm.at[x], left_out.at[x, c], dl_recv.at[0])
    dr_own = local(rterm.at[x], right_out.at[x, c], dr_recv.at[0])
    for k in RING:
        dlx(k).start()
    dl_own.start()
    py(OUT_ORDER[1]).wait_recv()
    send_z(OUT_ORDER[1])
    n_step(1)

    piece = width // NC

    def turn(i, carry):
        g = whole[:, :, :, :, cols(i * NC + c, piece)].reshape(order, piece)
        cols_t[pl.ds(pl.multiple_of(i * piece, piece), piece), :] = g.T
        return carry

    lax.fori_loop(0, NX, turn, 0)

    def gram_right(n, carry):
        g = whole[:, :, :, :, cols(n)].reshape(order, width)
        term = (factor * dot(cols_t[...], g, ((1,), (0,)))).astype(LOW)
        rterm[:, :, cols(n)] = term.reshape(NX, piece, width)
        return carry

    lax.fori_loop(0, tiles, gram_right, 0)
    for k in RING:
        drx(k).start()
    dr_own.start()
    for m in OUT_ORDER[2:]:
        py(m).wait_recv()
        send_z(m)
    n_step(2)

    def df(side, k):
        part = (left_out, right_out)[side].at[(x - k + NX) % NX, c]
        return remote(part, part, df_send.at[side, k], df_recv.at[side, k], sibling)

    dl_own.wait()
    df(0, 0).start()
    dr_own.wait()
    df(1, 0).start()
    for k in RING:
        dlx(k).wait_recv()
        df(0, k).start()
    n_step(3)
    for m in OUT_ORDER:
        for k in Z_ORDER:
            pz(m, k).wait_recv()
        pz_own(m).wait()

    def split(i, carry):
        rows_of = back[table[36 + i]]
        for t in range(NX):
            xs[t, i] = rows_of[:, t * width : (t + 1) * width]
        return carry

    lax.fori_loop(0, per_worker, split, 0)

    def px(k):
        to = (x + k) % NX
        return remote(xs.at[to], fin.at[x], px_send.at[k], px_recv.at[k], (to, y, z, c))

    px_own = local(xs.at[x], fin.at[x], px_recv.at[0])
    for k in RING:
        px(k).start()
    px_own.start()
    for k in RING:
        drx(k).wait_recv()
        df(1, k).start()
    n_step(4)
    px_own.wait()
    for k in RING:
        px(k).wait()
        gx(k).wait_send()
        lx(k).wait_send()
        rx(k).wait_send()
        gy(k).wait_send()
        py(k).wait_send()
        dlx(k).wait_send()
        drx(k).wait_send()
    for s in range(2):
        a, b, _, _ = exchange(s)
        a.wait_send()
        b.wait_send()
    for m in range(NY):
        for k in Z_ORDER:
            gz(m, k).wait_send()
            pz(m, k).wait_send()
        gc(m).wait_send()
        forward(m).wait_send()
        df(0, m).wait()
        df(1, m).wait()
    for stage in range(4):
        for copy in n_copies(stage):
            copy.wait_send()


def tail_kernel(
    table, place, flat, fin, rows, left_term, right_term, left_stat, right_stat,
    update, left_new, right_new, total,
):
    step = pl.program_id(0)
    blocks = update.shape[0]

    @pl.when(step == 0)
    def _():
        adam = jnp.sum(rows[:, 0:1, :], axis=0)
        total[...] = jnp.broadcast_to(adam, (128, 128)).T

    def apply(b, carry):
        index = step * blocks + b
        rank = place[index]
        worker = (flat[index] // NX) * NX + rank % NX
        root = rows[worker, 1:2, :] + rows[worker + NZ * NY * NX, 1:2, :]
        scale = jnp.sqrt(total[pl.ds(index, 1), :] / (root + 1e-06))
        wide = fin[rank % NX, rank // NX].astype(FULL)
        scale = jnp.concatenate([scale, scale], axis=1)
        update[b] = (wide * scale).astype(LOW)
        return carry

    lax.fori_loop(0, blocks, apply, 0)
    keep = jnp.where(table[48 + step // 4] > 0, 1, 0)
    for h in range(NC):
        term = jnp.where(keep > 0, left_term[0, h].astype(FULL), 0.0)
        left_new[0, :, h] = 0.5 * left_stat[0, :, h] + term
    right_new[0] = 0.5 * right_stat[0] + jnp.where(keep > 0, right_term[0].astype(FULL), 0.0)


ANY = pl.BlockSpec(memory_space=pl.ANY)
VMEM = pl.BlockSpec(memory_space=pltpu.VMEM)
DMA = pltpu.SemaphoreType.DMA


def tables(flat):
    x, y, z, c = position()
    rank = jnp.sum((flat[None, :] < flat[:, None]).astype(jnp.int32), axis=1)
    j = jnp.arange(64, dtype=jnp.int32)[:, None]
    f, r = flat[None, :], rank[None, :]
    chip = z * NY + y
    a = (f // 4 == j) & (r % NX == x)
    b = (f // 4 == chip) & (r % NX == j - 32)
    d = r == (j - 36) * NX + x
    e = f == (chip * NC + c) * 2 + j - 48
    value = jnp.where(
        j < 32,
        jnp.where(a, r // NX, 0),
        jnp.where(
            j < 36,
            jnp.where(b, f % 4, 0),
            jnp.where(j < 48, jnp.where(d, f // 4, 0), jnp.where(e & (j < 50), r % NX + 4, 0)),
        ),
    )
    return rank, jnp.sum(value, axis=1)


def per_device(
    gradient, second_moment, owner_table, slot_table, left_stat, right_stat, left_root, right_root
):
    blocks, rows, width = gradient.shape
    order = left_stat.shape[3]
    stripe = left_stat.shape[2]
    flat = owner_table * 2 + slot_table
    rank, table = tables(flat)
    each = blocks // NX
    groups = stripe // (NC * rows)
    shape = jax.ShapeDtypeStruct
    steps = 3
    block3 = pl.BlockSpec((blocks // steps, rows, width), lambda i, *_: (i, 0, 0))
    new_second, send, adam_row = pl.pallas_call(
        front_kernel,
        out_shape=(
            shape(gradient.shape, FULL),
            shape((NX, each, rows, width), LOW),
            shape((1, 128), FULL),
        ),
        grid_spec=pltpu.PrefetchScalarGridSpec(
            num_scalar_prefetch=1,
            grid=(steps,),
            in_specs=[block3, block3],
            out_specs=(
                block3,
                pl.BlockSpec((NX, each, rows, width), lambda i, *_: (0, 0, 0, 0)),
                pl.BlockSpec((1, 128), lambda i, *_: (0, 0)),
            ),
        ),
        name="front",
    )(rank, gradient, second_moment)

    half = order // NC
    fin, left_term, right_term, all_rows = pl.pallas_call(
        step_kernel,
        out_shape=(
            shape((NX, each, rows, width), LOW),
            shape((NX, NC, groups, rows, order), LOW),
            shape((NX, NC, stripe // NC, order), LOW),
            shape((NC, NZ, NY, NX, 2, 128), FULL),
        ),
        in_specs=[pl.BlockSpec(memory_space=pltpu.SMEM), ANY, ANY, ANY, VMEM],
        out_specs=(ANY,) * 4,
        scratch_shapes=[
            pltpu.VMEM((each, rows, order), LOW),
            pltpu.VMEM((NY, NZ, rows, order), LOW),
            pltpu.VMEM((NY, NZ, rows, order), LOW),
            pltpu.VMEM((NZ, NY, NC, rows, order), LOW),
            pltpu.VMEM((4, groups, rows, order), LOW),
            pltpu.VMEM((NX, groups, rows, order), LOW),
            pltpu.VMEM((NX, groups, rows, order), LOW),
            pltpu.VMEM((4, stripe // NC, order), LOW),
            pltpu.VMEM((NX, stripe // NC, order), LOW),
            pltpu.VMEM((NX, NC, stripe // NC, order), LOW),
            pltpu.VMEM((half, order), LOW),
            pltpu.VMEM((NZ, NY, rows, order), LOW),
            pltpu.VMEM((NY, NZ, rows, order), LOW),
            pltpu.VMEM((NZ * NY, rows, order), LOW),
            pltpu.VMEM((NX, each, rows, width), LOW),
            pltpu.VMEM((half, order), LOW),
            pltpu.VMEM((NX, groups, rows, order), LOW),
            pltpu.VMEM((NX, stripe // NC, order), LOW),
            pltpu.VMEM((2, 128), FULL),
            DMA((NX,)), DMA((NX,)), DMA((NY, NZ)), DMA((NY, NZ)),
            DMA((NY,)), DMA((NY,)), DMA((NY,)), DMA((NY,)),
            DMA((2, 2)), DMA((4, 2)), DMA((NX,)), DMA((NX,)), DMA((NX,)), DMA((NX,)),
            DMA((NX,)), DMA((NX,)),
            DMA((NY,)), DMA((NY,)), DMA((NY, NZ)), DMA((NY, NZ)), DMA((NX,)), DMA((NX,)),
            DMA((NX,)), DMA((NX,)), DMA((NX,)), DMA((NX,)), DMA((2, NX)), DMA((2, NX)),
            DMA((4, NZ)), DMA((4, NZ)),
        ],
        compiler_params=pltpu.CompilerParams(
            collective_id=0, has_side_effects=True, vmem_limit_bytes=48 << 20
        ),
        name="exchange_and_multiply",
    )(
        table,
        send,
        left_root.reshape(2, groups, NC, rows, order),
        right_root.reshape(2, NC, stripe // NC, order),
        adam_row,
    )

    steps = 8
    quarter = steps // 2
    part = blocks // steps

    def whole_spec(*dims):
        return pl.BlockSpec(dims, lambda i, *_: (0,) * len(dims))

    stat5 = pl.BlockSpec(
        (1, groups // quarter, NC, rows, order), lambda i, *_: (i // quarter, i % quarter, 0, 0, 0)
    )
    stat3 = pl.BlockSpec((1, stripe // quarter, order), lambda i, *_: (i // quarter, i % quarter, 0))
    update, left_new, right_new = pl.pallas_call(
        tail_kernel,
        out_shape=(
            shape(gradient.shape, LOW),
            shape((2, groups, NC, rows, order), FULL),
            shape((2, stripe, order), FULL),
        ),
        grid_spec=pltpu.PrefetchScalarGridSpec(
            num_scalar_prefetch=3,
            grid=(steps,),
            in_specs=[
                whole_spec(NX, each, rows, width),
                whole_spec(NC * NZ * NY * NX, 2, 128),
                pl.BlockSpec(
                    (1, NC, groups // quarter, rows, order),
                    lambda i, table, *_: (table[48 + i // quarter] % 4, 0, i % quarter, 0, 0),
                ),
                pl.BlockSpec(
                    (1, stripe // quarter, order),
                    lambda i, table, *_: (table[48 + i // quarter] % 4, i % quarter, 0),
                ),
                stat5,
                stat3,
            ],
            out_specs=(
                pl.BlockSpec((part, rows, width), lambda i, *_: (i, 0, 0)),
                stat5,
                stat3,
            ),
            scratch_shapes=[pltpu.VMEM((128, 128), FULL)],
        ),
        name="tail",
    )(
        table,
        rank,
        flat,
        fin,
        all_rows.reshape(NC * NZ * NY * NX, 2, 128),
        left_term,
        right_term.reshape(NX, stripe, order),
        left_stat.reshape(2, groups, NC, rows, order),
        right_stat.reshape(2, stripe, order),
    )
    return (
        update,
        new_second,
        left_new.reshape(left_stat.shape),
        right_new.reshape(right_stat.shape),
    )


def solution(mesh):
    placed = (
        P(None, "dp", "tensor"),
        P(None, "dp", "tensor"),
        P(),
        P(),
        P("dp", None, "tensor", None),
        P("dp", None, "tensor", None),
        P("dp", None, "tensor", None),
        P("dp", None, "tensor", None),
    )
    return jax.shard_map(
        per_device,
        mesh=mesh,
        in_specs=placed,
        out_specs=(
            P(None, "dp", "tensor"),
            P(None, "dp", "tensor"),
            P("dp", None, "tensor", None),
            P("dp", None, "tensor", None),
        ),
        check_vma=False,
    )
```
